32 devices in a mesh: grp: 4 (over x, core), uly: 8 (over z, y).
Axes of the slice: x: 2, y: 2, z: 4, core: 2. Of those that a mesh axis runs over, the one named last changes fastest.
Arguments:
- queries: bfloat16 [4096, 8192], P(('grp', 'uly')), may hold values from -6 to 6
- key_state_rows: bfloat16 [4096, 1024], P(('grp', 'uly')), may hold values from -6 to 6
- value_state_rows: bfloat16 [4096, 1024], P(('grp', 'uly')), may hold values from -6 to 6
- vert_blocks: int32 [64, 6], replicated, may hold values from -1 to 31, as said below
- slash_offsets: int32 [64, 3], replicated, may hold values from -1 to 4, as said below
Outputs:
- attended: bfloat16 [4096, 8192], P(('grp', 'uly'))
The draws below stay inside these ranges and needn't reach their ends.
Inputs may be any that keep to these rules, and one draw needn't show every extreme that they name: `vert_blocks`: row h lists distinct block numbers first and -1 in the slots after them; every row lists one block or more and some row lists 6. `slash_offsets`: row h lists distinct offsets of at least 1 first and -1 in the slots after them; every row lists one offset or more and some row lists 3.
All inputs are finite; a program needn't handle non-finite values.
Results may differ from the reference program's by a relative error of at most 0.005.
Values may be sent and summed in bfloat16 or wider, within the bound.
A program may use at most 128 MiB of HBM per device.

```python
import jax
import jax.numpy as jnp
from jax import lax

QUERY_HEADS = 64
KEY_VALUE_HEADS = 8
HEAD_SIZE = 128
BLOCK_TOKENS = 128
NV = 6
NS = 3
TOTAL_TOKENS = 4096
NBLK = 32
SPAN = 4


def draw_queries(key, part):
    random_jitter = jax.random.normal(jax.random.fold_in(key, 1), (TOTAL_TOKENS, QUERY_HEADS, HEAD_SIZE), dtype=jnp.float32)
    random_jitter = jnp.clip(random_jitter, -6.0, 6.0)
    return random_jitter.reshape(TOTAL_TOKENS, QUERY_HEADS * HEAD_SIZE).astype(jnp.bfloat16)


def draw_key_state_rows(key, part):
    random_jitter = jax.random.normal(jax.random.fold_in(key, 2), (TOTAL_TOKENS, KEY_VALUE_HEADS, HEAD_SIZE), dtype=jnp.float32)
    random_jitter = jnp.clip(random_jitter, -6.0, 6.0)
    return random_jitter.reshape(TOTAL_TOKENS, KEY_VALUE_HEADS * HEAD_SIZE).astype(jnp.bfloat16)


def draw_vert_blocks(key, part):
    head_keys = jax.random.split(jax.random.fold_in(key, 11), QUERY_HEADS)

    def pick_blocks(head_key):
        return jax.random.permutation(head_key, NBLK)[:NV]
    picks = jax.vmap(pick_blocks)(head_keys).astype(jnp.int32)
    heavy = jax.random.randint(jax.random.fold_in(key, 12), (QUERY_HEADS,), 0, 4) == 0
    lighter = jax.random.randint(jax.random.fold_in(key, 13), (QUERY_HEADS,), 1, 3)
    full_head = jax.random.randint(jax.random.fold_in(key, 14), (), 0, QUERY_HEADS)
    counts = jnp.where(heavy | (jnp.arange(QUERY_HEADS) == full_head), NV, lighter)
    return jnp.where(jnp.arange(NV)[None, :] < counts[:, None], picks, -1).astype(jnp.int32)


def draw_slash_offsets(key, part):
    head_keys = jax.random.split(jax.random.fold_in(key, 21), QUERY_HEADS)

    def pick_offsets(head_key):
        return jax.random.permutation(head_key, SPAN)[:NS] + 1
    picks = jax.vmap(pick_offsets)(head_keys).astype(jnp.int32)
    counts = jax.random.randint(jax.random.fold_in(key, 22), (QUERY_HEADS,), 1, NS + 1)
    full_head = jax.random.randint(jax.random.fold_in(key, 23), (), 0, QUERY_HEADS)
    counts = jnp.where(jnp.arange(QUERY_HEADS) == full_head, NS, counts)
    return jnp.where(jnp.arange(NS)[None, :] < counts[:, None], picks, -1).astype(jnp.int32)


def steps_of(stream_key, extent, cuts, low, top_value):
    level = 1.0
    for position, blocks in cuts:
        draws = jax.random.uniform(jax.random.fold_in(jax.random.fold_in(stream_key, 6), position), (blocks,), jnp.float32, low / len(cuts), top_value / len(cuts))
        level = level * jnp.repeat(jnp.exp(draws), extent[position] // blocks).reshape((-1,) + (1,) * (len(extent) - 1 - position))
    return level


def gaussian(key, shape, width, limit, cuts=(), kind=jnp.bfloat16):
    values = width * jax.random.normal(key, shape, jnp.float32)
    if cuts:
        values = values * steps_of(key, shape, cuts, -0.22, 0.18)
    return jnp.clip(values, -limit, limit).astype(kind)


def setup_inputs(seed: int = 0) -> dict:
    streams_of = jax.random.split(jax.random.key(seed), 6)
    return {
        "queries": draw_queries(jax.random.fold_in(streams_of[5], 71), 0),
        "key_state_rows": draw_key_state_rows(jax.random.fold_in(streams_of[5], 71), 0),
        "value_state_rows": gaussian(streams_of[2], (TOTAL_TOKENS, KEY_VALUE_HEADS * HEAD_SIZE), 1.0, 6.0, ((0, 32),)),
        "vert_blocks": draw_vert_blocks(jax.random.fold_in(streams_of[5], 71), 0),
        "slash_offsets": draw_slash_offsets(jax.random.fold_in(streams_of[5], 71), 0),
    }


neg_large = -1.0e30


def reference(queries, key_state_rows, value_state_rows, vert_blocks, slash_offsets):
    group_width = QUERY_HEADS // KEY_VALUE_HEADS
    total_blocks = TOTAL_TOKENS // BLOCK_TOKENS
    score_scale = HEAD_SIZE ** -0.5
    q_tiles = queries.reshape(total_blocks, BLOCK_TOKENS, QUERY_HEADS, HEAD_SIZE)
    key_block_tiles = key_state_rows.reshape(total_blocks, BLOCK_TOKENS, KEY_VALUE_HEADS, HEAD_SIZE)
    value_block_tiles = value_state_rows.reshape(total_blocks, BLOCK_TOKENS, KEY_VALUE_HEADS, HEAD_SIZE)
    blocks = jnp.arange(total_blocks, dtype=jnp.int32)
    causal = jnp.arange(BLOCK_TOKENS)[:, None] >= jnp.arange(BLOCK_TOKENS)[None, :]
    slot_total = 1 + NS + NV
    first_slot = jnp.arange(slot_total) == 0

    def one_head(head_index):
        kv_head = head_index // group_width
        q_head = lax.dynamic_index_in_dim(q_tiles, head_index, axis=2, keepdims=False).astype(jnp.float32)
        k_head = lax.dynamic_index_in_dim(key_block_tiles, kv_head, axis=2, keepdims=False)
        v_head = lax.dynamic_index_in_dim(value_block_tiles, kv_head, axis=2, keepdims=False)
        offset_list = lax.dynamic_index_in_dim(slash_offsets, head_index, axis=0, keepdims=False)
        vert_list = lax.dynamic_index_in_dim(vert_blocks, head_index, axis=0, keepdims=False)
        targets = blocks[:, None] - offset_list[None, :]
        slash_ok = (offset_list[None, :] >= 1) & (targets >= 0)
        hits = slash_ok[:, :, None] & (targets[:, :, None] == vert_list[None, None, :])
        vert_ok = (vert_list[None, :] >= 0) & (vert_list[None, :] < blocks[:, None]) & jnp.logical_not(jnp.any(hits, axis=1))
        vert_full = jnp.broadcast_to(vert_list[None, :], (total_blocks, NV))
        chosen = jnp.concatenate([blocks[:, None], jnp.where(slash_ok, targets, 0), jnp.where(vert_ok, vert_full, 0)], axis=1).astype(jnp.int32)
        allowed = jnp.concatenate([jnp.ones((total_blocks, 1), dtype=bool), slash_ok, vert_ok], axis=1)
        k_sel = k_head[chosen].astype(jnp.float32)
        v_sel = v_head[chosen].astype(jnp.float32)
        scores = jnp.einsum("nqd,nskd->nqsk", q_head, k_sel) * score_scale
        keep_mask = allowed[:, None, :, None] & (causal[None, :, None, :] | jnp.logical_not(first_slot)[None, None, :, None])
        scores = jnp.where(keep_mask, scores, neg_large)
        row_best = jnp.max(scores, axis=(2, 3), keepdims=True)
        weights = jnp.where(keep_mask, jnp.exp(scores - row_best), 0.0)
        total = jnp.sum(weights, axis=(2, 3))
        probs_low = weights.astype(jnp.bfloat16).astype(jnp.float32)
        summed = jnp.einsum("nqsk,nskd->nqd", probs_low, v_sel)
        return (summed / total[:, :, None]).astype(jnp.bfloat16)

    heads_out = lax.map(one_head, jnp.arange(QUERY_HEADS, dtype=jnp.int32))
    return heads_out.transpose(1, 2, 0, 3).reshape(TOTAL_TOKENS, QUERY_HEADS * HEAD_SIZE)
```

```python
import functools

import jax
import jax.numpy as jnp
import numpy as np
from jax import lax
from jax.experimental import pallas as pl
from jax.experimental.pallas import tpu as pltpu
from jax.sharding import PartitionSpec as P

QUERY_HEADS = 64
KEY_VALUE_HEADS = 8
HEAD_SIZE = 128
BLOCK_TOKENS = 128


neg_large = -1e30


def passed_along(value, axis, steps):
    count = lax.axis_size(axis)
    initial, last = (max(0, -steps), min(count, count - steps))
    return lax.ppermute(value, axis, [(source, source + steps) for source in range(initial, last)])


def add_slot(running, slot_scores, allowed, weigh):
    best, total, accum = running
    slot_scores = jnp.where(allowed, slot_scores, neg_large)
    new_best = jnp.maximum(best, jnp.max(slot_scores, axis=-1))
    factor = jnp.exp(best - new_best)
    weights = jnp.where(allowed, jnp.exp(slot_scores - new_best[..., None]), 0.0)
    total = total * factor + jnp.sum(weights, axis=-1)
    accum = accum * factor[..., None] + weigh(weights.astype(jnp.bfloat16))
    return (new_best, total, accum)


def shards(queries, key_state_rows, value_state_rows, vert_blocks, slash_offsets):
    ulysses_count = lax.axis_size("uly")
    group_id = lax.axis_index("grp")
    uly_id = lax.axis_index("uly")
    per_device = QUERY_HEADS // ulysses_count
    group_width = QUERY_HEADS // KEY_VALUE_HEADS
    token_rows = queries.shape[0]
    ordering = jnp.arange(QUERY_HEADS, dtype=jnp.int32)
    heads_per_slot = np.arange(ulysses_count) * per_device // group_width
    key_outgoing = key_state_rows.reshape(token_rows, KEY_VALUE_HEADS, HEAD_SIZE)[
        :, heads_per_slot
    ].reshape(token_rows, ulysses_count * HEAD_SIZE)
    value_outgoing = value_state_rows.reshape(token_rows, KEY_VALUE_HEADS, HEAD_SIZE)[
        :, heads_per_slot
    ].reshape(token_rows, ulysses_count * HEAD_SIZE)
    q_group, k_group, v_group = (
        lax.all_to_all(queries, "uly", split_axis=1, concat_axis=0, tiled=True),
        lax.all_to_all(key_outgoing, "uly", split_axis=1, concat_axis=0, tiled=True),
        lax.all_to_all(value_outgoing, "uly", split_axis=1, concat_axis=0, tiled=True),
    )
    seg_rows = q_group.shape[0]
    block_count = seg_rows // BLOCK_TOKENS
    reach = block_count // 2
    q_tiles = q_group.reshape(block_count, BLOCK_TOKENS, per_device, HEAD_SIZE)
    key_block_tiles = k_group.reshape(block_count, BLOCK_TOKENS, HEAD_SIZE)
    value_block_tiles = v_group.reshape(block_count, BLOCK_TOKENS, HEAD_SIZE)
    prior_k, prior_v = passed_along(
        (key_block_tiles[block_count - reach :], value_block_tiles[block_count - reach :]), "grp", 1
    )
    k_wide = jnp.concatenate([prior_k, key_block_tiles], axis=0)
    v_wide = jnp.concatenate([prior_v, value_block_tiles], axis=0)
    heads_here = lax.dynamic_slice_in_dim(ordering, uly_id * per_device, per_device)
    vert_list = jnp.take(vert_blocks, heads_here, axis=0)
    offset_list = jnp.take(slash_offsets, heads_here, axis=0)
    local_block = jnp.where(vert_list >= 0, vert_list % block_count, 0)
    owned = (vert_list >= 0) & (vert_list // block_count == group_id)
    pick_k = jnp.where(
        owned[:, :, None, None], key_block_tiles[local_block], jnp.zeros((), jnp.bfloat16)
    )
    pick_v = jnp.where(
        owned[:, :, None, None], value_block_tiles[local_block], jnp.zeros((), jnp.bfloat16)
    )
    summed_k, summed_v = (
        lax.psum(pick_k.astype(jnp.float32).astype(jnp.bfloat16), "grp").astype(jnp.float32),
        lax.psum(pick_v.astype(jnp.float32).astype(jnp.bfloat16), "grp").astype(jnp.float32),
    )
    vert_k = summed_k.astype(jnp.bfloat16)
    vert_v = summed_v.astype(jnp.bfloat16)
    query_blocks = group_id * block_count + jnp.arange(block_count, dtype=jnp.int32)
    score_scale = HEAD_SIZE ** (-0.5)
    causal = (jnp.arange(BLOCK_TOKENS)[:, None] >= jnp.arange(BLOCK_TOKENS)[None, :])[
        None, :, None, :
    ]
    diag_scores = (
        jnp.einsum("nqhd,nkd->nqhk", q_tiles, key_block_tiles, preferred_element_type=jnp.float32)
        * score_scale
    )
    diag_scores = jnp.where(causal, diag_scores, neg_large)
    best = jnp.max(diag_scores, axis=-1)
    diag_weights = jnp.where(causal, jnp.exp(diag_scores - best[..., None]), 0.0)
    total = jnp.sum(diag_weights, axis=-1)
    accum = jnp.einsum(
        "nqhk,nkd->nqhd",
        diag_weights.astype(jnp.bfloat16),
        value_block_tiles,
        preferred_element_type=jnp.float32,
    )
    running = (best, total, accum)

    def slash_slot(slot_index, running):
        offset_now = lax.dynamic_index_in_dim(offset_list, slot_index, axis=1, keepdims=False)
        starts = jnp.where(offset_now >= 1, reach - offset_now, 0)

        def near_slice(begin_at):
            return (
                lax.dynamic_slice_in_dim(k_wide, begin_at, block_count, 0),
                lax.dynamic_slice_in_dim(v_wide, begin_at, block_count, 0),
            )

        k_near, v_near = jax.vmap(near_slice)(starts)
        allowed = (offset_now[None, :] >= 1) & (query_blocks[:, None] - offset_now[None, :] >= 0)
        slot_scores = (
            jnp.einsum("nqhd,hnkd->nqhk", q_tiles, k_near, preferred_element_type=jnp.float32)
            * score_scale
        )

        def weigh_near(prob_low):
            return jnp.einsum(
                "nqhk,hnkd->nqhd", prob_low, v_near, preferred_element_type=jnp.float32
            )

        return add_slot(running, slot_scores, allowed[:, None, :, None], weigh_near)

    slash_turns = jnp.max(jnp.sum((offset_list >= 1).astype(jnp.int32), axis=1))
    running = lax.fori_loop(0, slash_turns, slash_slot, running)

    def vert_slot(slot_index, running):
        block_now = lax.dynamic_index_in_dim(vert_list, slot_index, axis=1, keepdims=False)
        k_far = lax.dynamic_index_in_dim(vert_k, slot_index, axis=1, keepdims=False)
        v_far = lax.dynamic_index_in_dim(vert_v, slot_index, axis=1, keepdims=False)
        hits = (offset_list[None, :, :] >= 1) & (
            query_blocks[:, None, None] - offset_list[None, :, :] == block_now[None, :, None]
        )
        allowed = (
            (block_now[None, :] >= 0)
            & (block_now[None, :] < query_blocks[:, None])
            & jnp.logical_not(jnp.any(hits, axis=2))
        )
        slot_scores = (
            jnp.einsum("nqhd,hkd->nqhk", q_tiles, k_far, preferred_element_type=jnp.float32)
            * score_scale
        )

        def weigh_far(prob_low):
            return jnp.einsum("nqhk,hkd->nqhd", prob_low, v_far, preferred_element_type=jnp.float32)

        return add_slot(running, slot_scores, allowed[:, None, :, None], weigh_far)

    vert_turns = jnp.max(jnp.sum((vert_list >= 0).astype(jnp.int32), axis=1))
    best, total, accum = lax.fori_loop(0, vert_turns, vert_slot, running)
    mixed = (
        (accum / total[..., None]).astype(jnp.bfloat16).reshape(seg_rows, per_device * HEAD_SIZE)
    )
    returned = lax.all_to_all(mixed, "uly", split_axis=0, concat_axis=1, tiled=True)
    return returned


MESH = pl.DeviceIdType.MESH
GATHERED_BYTES_MAX = 1 << 25
LOG2_E = 1.4426950408889634


def block_places(group_count, uly_count):
    x_count, z_count = group_count // 2, uly_count // 2
    block = np.arange(group_count * uly_count)
    group, member = block // uly_count, block % uly_count
    x, core, z, y = group // 2, group % 2, member // 2, member % 2
    key_place = ((core * x_count + x) * 2 + y) * z_count + z
    value_place = ((core * 2 + y) * x_count + x) * z_count + z
    return key_place.astype(np.int32), value_place.astype(np.int32)


def gather_kernel(
    group_count, uly_count, k_ref, v_ref, k_out, v_out, own_sem, send_sem, recv_sem
):
    x_count, z_count = group_count // 2, uly_count // 2
    group, member = lax.axis_index("grp"), lax.axis_index("uly")
    x, core = group // 2, group % 2
    z, y = member // 2, member % 2
    heads = k_out.shape[0]

    z_peers = [(group, lax.rem(z + d, z_count) * 2 + y) for d in range(1, z_count)]
    y_peers = [(group, z * 2 + 1 - y)]
    x_peers = [(lax.rem(x + d, x_count) * 2 + core, member) for d in range(1, x_count)]
    core_peers = [(x * 2 + 1 - core, member)]
    first_x = z_count - 1
    first_y = first_x + x_count - 1
    first_core = first_y + 1

    barrier = pltpu.get_barrier_semaphore()
    everyone = z_peers + y_peers + x_peers + core_peers
    for peer in everyone:
        pl.semaphore_signal(barrier, inc=1, device_id=peer, device_id_type=MESH)
    pl.semaphore_wait(barrier, len(everyone))

    def remote(source, target, item, number, peer):
        return pltpu.make_async_remote_copy(
            src_ref=source,
            dst_ref=target,
            send_sem=send_sem.at[item, number],
            recv_sem=recv_sem.at[item, number],
            device_id=peer,
            device_id_type=MESH,
        )

    k_own = ((core * x_count + x) * 2 + y) * z_count + z
    v_own = ((core * 2 + y) * x_count + x) * z_count + z
    all_copies = []

    def slab_copies(out, head, item, start, count, first, peers):
        slab = out.at[head, pl.ds(start, count)]
        return [remote(slab, slab, item, first + n, peer) for n, peer in enumerate(peers)]

    own, along_z = [], []
    for head in range(heads):
        for item, source, out, place in (
            (2 * head, k_ref, k_out, k_own),
            (2 * head + 1, v_ref, v_out, v_own),
        ):
            columns = source.at[:, pl.ds(head * HEAD_SIZE, HEAD_SIZE)]
            slot = out.at[head, place]
            local = pltpu.make_async_copy(columns, slot, own_sem.at[item])
            sends = [remote(columns, slot, item, n, peer) for n, peer in enumerate(z_peers)]
            for copy in sends:
                copy.start()
            local.start()
            own.append(local)
            along_z.append(sends)
            all_copies += sends

    second, third, fourth = {}, {}, {}

    def started(copies):
        for copy in copies:
            copy.start()
        all_copies.extend(copies)
        return copies

    def arrived(copies):
        for copy in copies:
            copy.wait_recv()

    for step in range(heads + 3):
        head = step
        if head < heads:
            k_item, v_item = 2 * head, 2 * head + 1
            own[k_item].wait()
            arrived(along_z[k_item])
            second[k_item] = started(
                slab_copies(k_out, head, k_item, k_own - z, z_count, first_y, y_peers)
            )
            own[v_item].wait()
            arrived(along_z[v_item])
            second[v_item] = started(
                slab_copies(v_out, head, v_item, v_own - z, z_count, first_x, x_peers)
            )
        head = step - 1
        if 0 <= head < heads:
            k_item, v_item = 2 * head, 2 * head + 1
            arrived(second[k_item])
            start = (core * x_count + x) * 2 * z_count
            third[k_item] = started(
                slab_copies(k_out, head, k_item, start, 2 * z_count, first_x, x_peers)
            )
            arrived(second[v_item])
            start = (core * 2 + y) * x_count * z_count
            third[v_item] = started(
                slab_copies(v_out, head, v_item, start, x_count * z_count, first_y, y_peers)
            )
        head = step - 2
        if 0 <= head < heads:
            half = 2 * x_count * z_count
            for item, out in ((2 * head, k_out), (2 * head + 1, v_out)):
                arrived(third[item])
                fourth[item] = started(
                    slab_copies(out, head, item, core * half, half, first_core, core_peers)
                )
        head = step - 3
        if 0 <= head < heads:
            arrived(fourth[2 * head])
            arrived(fourth[2 * head + 1])
    for copy in all_copies:
        copy.wait_send()


def gathered(key_rows, value_rows, group_count, uly_count):
    blocks = group_count * uly_count
    shape = jax.ShapeDtypeStruct(
        (KEY_VALUE_HEADS, blocks, BLOCK_TOKENS, HEAD_SIZE), key_rows.dtype
    )
    copies = uly_count // 2 - 1 + group_count // 2 - 1 + 2
    items = 2 * KEY_VALUE_HEADS
    return pl.pallas_call(
        functools.partial(gather_kernel, group_count, uly_count),
        out_shape=(shape, shape),
        in_specs=[pl.BlockSpec(memory_space=pltpu.VMEM)] * 2,
        out_specs=(pl.BlockSpec(memory_space=pl.ANY),) * 2,
        scratch_shapes=[
            pltpu.SemaphoreType.DMA((items,)),
            pltpu.SemaphoreType.DMA((items, copies)),
            pltpu.SemaphoreType.DMA((items, copies)),
        ],
        compiler_params=pltpu.CompilerParams(collective_id=0, has_side_effects=True),
        name="gather_blocks",
    )(key_rows, value_rows)


def attend_kernel(
    variants,
    here_ref,
    key_place,
    value_place,
    vert_ref,
    slash_ref,
    q_ref,
    k_ref,
    v_ref,
    out_ref,
    held,
    counts,
):
    kv_head = pl.program_id(0)
    per_group = q_ref.shape[1] // HEAD_SIZE
    slash_slots, vert_slots = slash_ref.shape[1], vert_ref.shape[1]
    here = here_ref[0]

    @pl.loop(0, per_group)
    def _(local):
        head = kv_head * per_group + local
        for slot in range(slash_slots + vert_slots):
            held[local, slot] = here
        filled = jnp.int32(0)
        offsets = [slash_ref[head, slot] for slot in range(slash_slots)]
        for offset in offsets:
            held[local, filled] = here - offset
            ok = (offset >= 1) & (here - offset >= 0)
            filled = filled + ok.astype(jnp.int32)
        for slot in range(vert_slots):
            block = vert_ref[head, slot]
            ok = (block >= 0) & (block < here)
            for offset in offsets:
                ok = ok & jnp.logical_not((offset >= 1) & (here - offset == block))
            held[local, filled] = block
            filled = filled + ok.astype(jnp.int32)
        counts[local] = filled

    rate = HEAD_SIZE ** (-0.5) * LOG2_E
    causal = lax.broadcasted_iota(
        jnp.int32, (BLOCK_TOKENS, BLOCK_TOKENS), 0
    ) >= lax.broadcasted_iota(jnp.int32, (BLOCK_TOKENS, BLOCK_TOKENS), 1)

    def attend(local, extra):
        columns = pl.ds(pl.multiple_of(local * HEAD_SIZE, HEAD_SIZE), HEAD_SIZE)
        q = q_ref[:, columns]
        filled = counts[local]
        blocks = [here]
        for slot in range(extra):
            blocks.append(jnp.where(slot < filled, held[local, slot], here))
        keys = jnp.concatenate([k_ref[0, key_place[block]] for block in blocks], axis=0)
        values = jnp.concatenate([v_ref[0, value_place[block]] for block in blocks], axis=0)
        scores = lax.dot_general(
            q, keys, (((1,), (1,)), ((), ())), preferred_element_type=jnp.float32
        )
        pieces = [
            scores[:, n * BLOCK_TOKENS : (n + 1) * BLOCK_TOKENS] for n in range(extra + 1)
        ]
        pieces[0] = jnp.where(causal, pieces[0], neg_large)
        for slot in range(extra):
            bias = jnp.where(slot < filled, 0.0, neg_large).astype(jnp.float32)
            pieces[slot + 1] = pieces[slot + 1] + bias
        best = pieces[0]
        for piece in pieces[1:]:
            best = jnp.maximum(best, piece)
        best = jnp.max(best, axis=1, keepdims=True)
        weights = [jnp.exp2((piece - best) * rate) for piece in pieces]
        total = weights[0]
        for weight in weights[1:]:
            total = total + weight
        total = jnp.sum(total, axis=1, keepdims=True)
        probs = jnp.concatenate([weight.astype(jnp.bfloat16) for weight in weights], axis=1)
        mixed = jnp.dot(probs, values, preferred_element_type=jnp.float32)
        out_ref[:, columns] = (mixed / total).astype(out_ref.dtype)

    @pl.loop(0, per_group // 2)
    def _(pair):
        one, two = 2 * pair, 2 * pair + 1
        most = jnp.maximum(counts[one], counts[two])
        below = -1
        for extra in variants:

            @pl.when((most > below) & (most <= extra))
            def _(extra=extra):
                attend(one, extra)
                attend(two, extra)

            below = extra


def attended_here(queries, keys, values, vert_blocks, slash_offsets, here, places):
    tokens, width = queries.shape
    blocks = keys.shape[1]
    per_group = QUERY_HEADS // KEY_VALUE_HEADS
    slots = vert_blocks.shape[1] + slash_offsets.shape[1]
    variants = sorted({min(n, slots) for n in range(1, slots + 2, 2)})
    wide = pl.BlockSpec((tokens, per_group * HEAD_SIZE), lambda n, *_: (0, n))
    held = pl.BlockSpec((1, blocks, BLOCK_TOKENS, HEAD_SIZE), lambda n, *_: (n, 0, 0, 0))
    return pl.pallas_call(
        functools.partial(attend_kernel, variants),
        out_shape=jax.ShapeDtypeStruct((tokens, width), queries.dtype),
        grid_spec=pltpu.PrefetchScalarGridSpec(
            num_scalar_prefetch=5,
            grid=(KEY_VALUE_HEADS,),
            in_specs=[wide, held, held],
            out_specs=wide,
            scratch_shapes=[
                pltpu.SMEM((per_group, slots + 1), jnp.int32),
                pltpu.SMEM((per_group,), jnp.int32),
            ],
        ),
        compiler_params=pltpu.CompilerParams(dimension_semantics=("arbitrary",)),
        name="attend_blocks",
    )(here, *places, vert_blocks, slash_offsets, queries, keys, values)


def resident_shards(queries, key_state_rows, value_state_rows, vert_blocks, slash_offsets):
    group_count, uly_count = lax.axis_size("grp"), lax.axis_size("uly")
    here = (lax.axis_index("grp") * uly_count + lax.axis_index("uly")).astype(jnp.int32)
    keys, values = gathered(key_state_rows, value_state_rows, group_count, uly_count)
    places = [jnp.asarray(place) for place in block_places(group_count, uly_count)]
    return attended_here(
        queries, keys, values, vert_blocks, slash_offsets, here.reshape(1), places
    )


def chosen(queries, key_state_rows, *rest):
    devices = lax.axis_size("grp") * lax.axis_size("uly")
    gathered_bytes = 2 * devices * key_state_rows.size * key_state_rows.dtype.itemsize
    fits = gathered_bytes <= GATHERED_BYTES_MAX and queries.shape[0] == BLOCK_TOKENS
    plan = resident_shards if fits else shards
    return plan(queries, key_state_rows, *rest)


def solution(mesh):
    return jax.shard_map(
        chosen,
        mesh=mesh,
        in_specs=(
            P(("grp", "uly"), None),
            P(("grp", "uly"), None),
            P(("grp", "uly"), None),
            P(),
            P(),
        ),
        out_specs=P(("grp", "uly"), None),
        check_vma=False,
    )
```

```python
import functools

import jax
import jax.numpy as jnp
import numpy as np
from jax import lax
from jax.experimental import pallas as pl
from jax.experimental.pallas import tpu as pltpu
from jax.sharding import PartitionSpec as P

QUERY_HEADS = 64
KEY_VALUE_HEADS = 8
HEAD_SIZE = 128
BLOCK_TOKENS = 128


neg_large = -1e30


def passed_along(value, axis, steps):
    count = lax.axis_size(axis)
    initial, last = (max(0, -steps), min(count, count - steps))
    return lax.ppermute(value, axis, [(source, source + steps) for source in range(initial, last)])


def add_slot(running, slot_scores, allowed, weigh):
    best, total, accum = running
    slot_scores = jnp.where(allowed, slot_scores, neg_large)
    new_best = jnp.maximum(best, jnp.max(slot_scores, axis=-1))
    factor = jnp.exp(best - new_best)
    weights = jnp.where(allowed, jnp.exp(slot_scores - new_best[..., None]), 0.0)
    total = total * factor + jnp.sum(weights, axis=-1)
    accum = accum * factor[..., None] + weigh(weights.astype(jnp.bfloat16))
    return (new_best, total, accum)


def shards(queries, key_state_rows, value_state_rows, vert_blocks, slash_offsets):
    ulysses_count = lax.axis_size("uly")
    group_id = lax.axis_index("grp")
    uly_id = lax.axis_index("uly")
    per_device = QUERY_HEADS // ulysses_count
    group_width = QUERY_HEADS // KEY_VALUE_HEADS
    token_rows = queries.shape[0]
    ordering = jnp.arange(QUERY_HEADS, dtype=jnp.int32)
    heads_per_slot = np.arange(ulysses_count) * per_device // group_width
    key_outgoing = key_state_rows.reshape(token_rows, KEY_VALUE_HEADS, HEAD_SIZE)[
        :, heads_per_slot
    ].reshape(token_rows, ulysses_count * HEAD_SIZE)
    value_outgoing = value_state_rows.reshape(token_rows, KEY_VALUE_HEADS, HEAD_SIZE)[
        :, heads_per_slot
    ].reshape(token_rows, ulysses_count * HEAD_SIZE)
    q_group, k_group, v_group = (
        lax.all_to_all(queries, "uly", split_axis=1, concat_axis=0, tiled=True),
        lax.all_to_all(key_outgoing, "uly", split_axis=1, concat_axis=0, tiled=True),
        lax.all_to_all(value_outgoing, "uly", split_axis=1, concat_axis=0, tiled=True),
    )
    seg_rows = q_group.shape[0]
    block_count = seg_rows // BLOCK_TOKENS
    reach = block_count // 2
    q_tiles = q_group.reshape(block_count, BLOCK_TOKENS, per_device, HEAD_SIZE)
    key_block_tiles = k_group.reshape(block_count, BLOCK_TOKENS, HEAD_SIZE)
    value_block_tiles = v_group.reshape(block_count, BLOCK_TOKENS, HEAD_SIZE)
    prior_k, prior_v = passed_along(
        (key_block_tiles[block_count - reach :], value_block_tiles[block_count - reach :]), "grp", 1
    )
    k_wide = jnp.concatenate([prior_k, key_block_tiles], axis=0)
    v_wide = jnp.concatenate([prior_v, value_block_tiles], axis=0)
    heads_here = lax.dynamic_slice_in_dim(ordering, uly_id * per_device, per_device)
    vert_list = jnp.take(vert_blocks, heads_here, axis=0)
    offset_list = jnp.take(slash_offsets, heads_here, axis=0)
    local_block = jnp.where(vert_list >= 0, vert_list % block_count, 0)
    owned = (vert_list >= 0) & (vert_list // block_count == group_id)
    pick_k = jnp.where(
        owned[:, :, None, None], key_block_tiles[local_block], jnp.zeros((), jnp.bfloat16)
    )
    pick_v = jnp.where(
        owned[:, :, None, None], value_block_tiles[local_block], jnp.zeros((), jnp.bfloat16)
    )
    summed_k, summed_v = (
        lax.psum(pick_k.astype(jnp.float32).astype(jnp.bfloat16), "grp").astype(jnp.float32),
        lax.psum(pick_v.astype(jnp.float32).astype(jnp.bfloat16), "grp").astype(jnp.float32),
    )
    vert_k = summed_k.astype(jnp.bfloat16)
    vert_v = summed_v.astype(jnp.bfloat16)
    query_blocks = group_id * block_count + jnp.arange(block_count, dtype=jnp.int32)
    score_scale = HEAD_SIZE ** (-0.5)
    causal = (jnp.arange(BLOCK_TOKENS)[:, None] >= jnp.arange(BLOCK_TOKENS)[None, :])[
        None, :, None, :
    ]
    diag_scores = (
        jnp.einsum("nqhd,nkd->nqhk", q_tiles, key_block_tiles, preferred_element_type=jnp.float32)
        * score_scale
    )
    diag_scores = jnp.where(causal, diag_scores, neg_large)
    best = jnp.max(diag_scores, axis=-1)
    diag_weights = jnp.where(causal, jnp.exp(diag_scores - best[..., None]), 0.0)
    total = jnp.sum(diag_weights, axis=-1)
    accum = jnp.einsum(
        "nqhk,nkd->nqhd",
        diag_weights.astype(jnp.bfloat16),
        value_block_tiles,
        preferred_element_type=jnp.float32,
    )
    running = (best, total, accum)

    def slash_slot(slot_index, running):
        offset_now = lax.dynamic_index_in_dim(offset_list, slot_index, axis=1, keepdims=False)
        starts = jnp.where(offset_now >= 1, reach - offset_now, 0)

        def near_slice(begin_at):
            return (
                lax.dynamic_slice_in_dim(k_wide, begin_at, block_count, 0),
                lax.dynamic_slice_in_dim(v_wide, begin_at, block_count, 0),
            )

        k_near, v_near = jax.vmap(near_slice)(starts)
        allowed = (offset_now[None, :] >= 1) & (query_blocks[:, None] - offset_now[None, :] >= 0)
        slot_scores = (
            jnp.einsum("nqhd,hnkd->nqhk", q_tiles, k_near, preferred_element_type=jnp.float32)
            * score_scale
        )

        def weigh_near(prob_low):
            return jnp.einsum(
                "nqhk,hnkd->nqhd", prob_low, v_near, preferred_element_type=jnp.float32
            )

        return add_slot(running, slot_scores, allowed[:, None, :, None], weigh_near)

    slash_turns = jnp.max(jnp.sum((offset_list >= 1).astype(jnp.int32), axis=1))
    running = lax.fori_loop(0, slash_turns, slash_slot, running)

    def vert_slot(slot_index, running):
        block_now = lax.dynamic_index_in_dim(vert_list, slot_index, axis=1, keepdims=False)
        k_far = lax.dynamic_index_in_dim(vert_k, slot_index, axis=1, keepdims=False)
        v_far = lax.dynamic_index_in_dim(vert_v, slot_index, axis=1, keepdims=False)
        hits = (offset_list[None, :, :] >= 1) & (
            query_blocks[:, None, None] - offset_list[None, :, :] == block_now[None, :, None]
        )
        allowed = (
            (block_now[None, :] >= 0)
            & (block_now[None, :] < query_blocks[:, None])
            & jnp.logical_not(jnp.any(hits, axis=2))
        )
        slot_scores = (
            jnp.einsum("nqhd,hkd->nqhk", q_tiles, k_far, preferred_element_type=jnp.float32)
            * score_scale
        )

        def weigh_far(prob_low):
            return jnp.einsum("nqhk,hkd->nqhd", prob_low, v_far, preferred_element_type=jnp.float32)

        return add_slot(running, slot_scores, allowed[:, None, :, None], weigh_far)

    vert_turns = jnp.max(jnp.sum((vert_list >= 0).astype(jnp.int32), axis=1))
    best, total, accum = lax.fori_loop(0, vert_turns, vert_slot, running)
    mixed = (
        (accum / total[..., None]).astype(jnp.bfloat16).reshape(seg_rows, per_device * HEAD_SIZE)
    )
    returned = lax.all_to_all(mixed, "uly", split_axis=0, concat_axis=1, tiled=True)
    return returned


MESH = pl.DeviceIdType.MESH
GATHERED_BYTES_MAX = 1 << 25
LOG2_E = 1.4426950408889634
EARLY = ("zyx", "zxy")
LATE = ("yzx", "xzy")


def orders_of(head):
    return LATE if head % 3 == 0 else EARLY


def place_in(order, sizes, where):
    place = where["core"]
    for axis in reversed(order):
        place = place * sizes[axis] + where[axis]
    return place


def sizes_of(group_count, uly_count):
    return {"x": group_count // 2, "core": 2, "y": 2, "z": uly_count // 2}


def whereabouts(group, member):
    return {"x": group // 2, "core": group % 2, "y": member % 2, "z": member // 2}


def place_table(group_count, uly_count):
    block = np.arange(group_count * uly_count)
    where = whereabouts(block // uly_count, block % uly_count)
    sizes = sizes_of(group_count, uly_count)
    rows = [place_in(order, sizes, where) for order in EARLY + LATE]
    return np.stack(rows).astype(np.int32)


def attend_all(orders, q_ref, k_buf, v_buf, place_ref, vert_ref, slash_ref, out_ref, head, here):
    per_group = q_ref.shape[1] // (HEAD_SIZE * KEY_VALUE_HEADS)
    slash_slots, vert_slots = slash_ref.shape[0], vert_ref.shape[0]
    rate = HEAD_SIZE ** (-0.5) * LOG2_E
    causal = lax.broadcasted_iota(
        jnp.int32, (BLOCK_TOKENS, BLOCK_TOKENS), 0
    ) >= lax.broadcasted_iota(jnp.int32, (BLOCK_TOKENS, BLOCK_TOKENS), 1)
    k_row, v_row = ((EARLY + LATE).index(order) for order in orders)

    def slots_of(q_head):
        blocks, allowed = [here], [None]
        offsets = [slash_ref[slot, q_head] for slot in range(slash_slots)]
        for offset in offsets:
            ok = (offset >= 1) & (here - offset >= 0)
            blocks.append(jnp.where(ok, here - offset, here))
            allowed.append(ok)
        for slot in range(vert_slots):
            block = vert_ref[slot, q_head]
            ok = (block >= 0) & (block < here)
            for offset in offsets:
                ok = ok & jnp.logical_not((offset >= 1) & (here - offset == block))
            blocks.append(jnp.where(ok, block, here))
            allowed.append(ok)
        return blocks, allowed

    @pl.loop(0, per_group // GANG)
    def _(turn):
        chosen_slots, columns, scores = [], [], []
        for n in range(GANG):
            q_head = head * per_group + GANG * turn + n
            columns.append(pl.ds(pl.multiple_of(q_head * HEAD_SIZE, HEAD_SIZE), HEAD_SIZE))
            chosen_slots.append(slots_of(q_head))
        for n in range(GANG):
            blocks, _ = chosen_slots[n]
            keys = jnp.concatenate([k_buf[place_ref[k_row, block]] for block in blocks], axis=0)
            scores.append(
                lax.dot_general(
                    q_ref[:, columns[n]],
                    keys,
                    (((1,), (1,)), ((), ())),
                    preferred_element_type=jnp.float32,
                )
            )
        probs, totals = [], []
        for n in range(GANG):
            _, allowed = chosen_slots[n]
            pieces = []
            for slot, ok in enumerate(allowed):
                piece = scores[n][:, slot * BLOCK_TOKENS : (slot + 1) * BLOCK_TOKENS]
                if ok is None:
                    pieces.append(jnp.where(causal, piece, neg_large))
                else:
                    pieces.append(piece + jnp.where(ok, 0.0, neg_large).astype(jnp.float32))
            best = functools.reduce(jnp.maximum, pieces)
            best = jnp.max(best, axis=1, keepdims=True)
            weights = [jnp.exp2((piece - best) * rate) for piece in pieces]
            total = functools.reduce(jnp.add, weights)
            totals.append(jnp.sum(total, axis=1, keepdims=True))
            probs.append(
                jnp.concatenate([weight.astype(jnp.bfloat16) for weight in weights], axis=1)
            )
        for n in range(GANG):
            blocks, _ = chosen_slots[n]
            values = jnp.concatenate([v_buf[place_ref[v_row, block]] for block in blocks], axis=0)
            mixed = jnp.dot(probs[n], values, preferred_element_type=jnp.float32)
            out_ref[:, columns[n]] = (mixed / totals[n]).astype(out_ref.dtype)


GANG = 2


def resident_kernel(
    group_count,
    uly_count,
    place_ref,
    vert_ref,
    slash_ref,
    q_ref,
    k_ref,
    v_ref,
    out_ref,
    own_sem,
    send_sem,
    recv_sem,
    *held,
):
    sizes = sizes_of(group_count, uly_count)
    group, member = lax.axis_index("grp"), lax.axis_index("uly")
    me = whereabouts(group, member)
    here = group * uly_count + member
    heads = KEY_VALUE_HEADS

    def device_at(where):
        return (where["x"] * 2 + where["core"], where["z"] * 2 + where["y"])

    peers, first, used = {}, {}, 0
    for axis in ("x", "y", "z", "core"):
        count = sizes[axis]
        peers[axis] = [
            device_at({**me, axis: lax.rem(me[axis] + d, count)}) for d in range(1, count)
        ]
        first[axis] = used
        used += count - 1

    barrier = pltpu.get_barrier_semaphore()
    everyone = [peer for group_peers in peers.values() for peer in group_peers]
    for peer in everyone:
        pl.semaphore_signal(barrier, inc=1, device_id=peer, device_id_type=MESH)
    pl.semaphore_wait(barrier, len(everyone))

    all_copies = []

    def sent(source, target, item, axis):
        copies = []
        for n, peer in enumerate(peers[axis]):
            copy = pltpu.make_async_remote_copy(
                src_ref=source,
                dst_ref=target,
                send_sem=send_sem.at[item, first[axis] + n],
                recv_sem=recv_sem.at[item, first[axis] + n],
                device_id=peer,
                device_id_type=MESH,
            )
            copy.start()
            copies.append(copy)
        all_copies.extend(copies)
        return copies

    flights, own = {}, {}
    for head in range(heads):
        for kind, source in enumerate((k_ref, v_ref)):
            item, order = 2 * head + kind, orders_of(head)[kind]
            slot = held[item].at[place_in(order, sizes, me)]
            columns = source.at[:, pl.ds(head * HEAD_SIZE, HEAD_SIZE)]
            flights[item] = sent(columns, slot, item, order[0])
            own[item] = pltpu.make_async_copy(columns, slot, own_sem.at[item])
            own[item].start()

    def forward(head, stage):
        for kind in range(2):
            item, order = 2 * head + kind, orders_of(head)[kind]
            if stage == 1:
                own[item].wait()
            for copy in flights[item]:
                copy.wait_recv()
            if stage <= 3:
                route = [*order, "core"]
                start = {**me, **{axis: 0 for axis in route[:stage]}}
                count = 1
                for axis in route[:stage]:
                    count *= sizes[axis]
                slab = held[item].at[pl.ds(place_in(order, sizes, start), count)]
                flights[item] = sent(slab, slab, item, route[stage])

    for step in range(heads + 3):
        if step < heads:
            forward(step, 1)
        if 0 <= step - 1 < heads:
            forward(step - 1, 2)
        if 0 <= step - 3 < heads:
            head = step - 3
            forward(head, 4)
            attend_all(
                orders_of(head),
                q_ref,
                held[2 * head],
                held[2 * head + 1],
                place_ref,
                vert_ref,
                slash_ref,
                out_ref,
                head,
                here,
            )
        if 0 <= step - 2 < heads:
            forward(step - 2, 3)
    for copy in all_copies:
        copy.wait_send()


def resident_shards(queries, key_state_rows, value_state_rows, vert_blocks, slash_offsets):
    group_count, uly_count = lax.axis_size("grp"), lax.axis_size("uly")
    sizes = sizes_of(group_count, uly_count)
    copies = sum(count - 1 for count in sizes.values())
    items = 2 * KEY_VALUE_HEADS
    blocks = group_count * uly_count
    vmem = pl.BlockSpec(memory_space=pltpu.VMEM)
    smem = pl.BlockSpec(memory_space=pltpu.SMEM)
    return pl.pallas_call(
        functools.partial(resident_kernel, group_count, uly_count),
        out_shape=jax.ShapeDtypeStruct(queries.shape, queries.dtype),
        in_specs=[smem, smem, smem, vmem, vmem, vmem],
        out_specs=vmem,
        scratch_shapes=[
            pltpu.SemaphoreType.DMA((items,)),
            pltpu.SemaphoreType.DMA((items, copies)),
            pltpu.SemaphoreType.DMA((items, copies)),
        ]
        + [pltpu.VMEM((blocks, BLOCK_TOKENS, HEAD_SIZE), key_state_rows.dtype)] * items,
        compiler_params=pltpu.CompilerParams(collective_id=0, has_side_effects=True),
        name="gather_and_attend",
    )(
        jnp.asarray(place_table(group_count, uly_count)),
        vert_blocks.T,
        slash_offsets.T,
        queries,
        key_state_rows,
        value_state_rows,
    )


def chosen(queries, key_state_rows, *rest):
    devices = lax.axis_size("grp") * lax.axis_size("uly")
    gathered_bytes = 2 * devices * key_state_rows.size * key_state_rows.dtype.itemsize
    fits = gathered_bytes <= GATHERED_BYTES_MAX and queries.shape[0] == BLOCK_TOKENS
    plan = resident_shards if fits else shards
    return plan(queries, key_state_rows, *rest)


def solution(mesh):
    return jax.shard_map(
        chosen,
        mesh=mesh,
        in_specs=(
            P(("grp", "uly"), None),
            P(("grp", "uly"), None),
            P(("grp", "uly"), None),
            P(),
            P(),
        ),
        out_specs=P(("grp", "uly"), None),
        check_vma=False,
    )
```

```python
import functools

import jax
import jax.numpy as jnp
import numpy as np
from jax import lax
from jax.experimental import pallas as pl
from jax.experimental.pallas import tpu as pltpu
from jax.sharding import PartitionSpec as P

QUERY_HEADS = 64
KEY_VALUE_HEADS = 8
HEAD_SIZE = 128
BLOCK_TOKENS = 128


neg_large = -1e30


def passed_along(value, axis, steps):
    count = lax.axis_size(axis)
    initial, last = (max(0, -steps), min(count, count - steps))
    return lax.ppermute(value, axis, [(source, source + steps) for source in range(initial, last)])


def add_slot(running, slot_scores, allowed, weigh):
    best, total, accum = running
    slot_scores = jnp.where(allowed, slot_scores, neg_large)
    new_best = jnp.maximum(best, jnp.max(slot_scores, axis=-1))
    factor = jnp.exp(best - new_best)
    weights = jnp.where(allowed, jnp.exp(slot_scores - new_best[..., None]), 0.0)
    total = total * factor + jnp.sum(weights, axis=-1)
    accum = accum * factor[..., None] + weigh(weights.astype(jnp.bfloat16))
    return (new_best, total, accum)


def shards(queries, key_state_rows, value_state_rows, vert_blocks, slash_offsets):
    ulysses_count = lax.axis_size("uly")
    group_id = lax.axis_index("grp")
    uly_id = lax.axis_index("uly")
    per_device = QUERY_HEADS // ulysses_count
    group_width = QUERY_HEADS // KEY_VALUE_HEADS
    token_rows = queries.shape[0]
    ordering = jnp.arange(QUERY_HEADS, dtype=jnp.int32)
    heads_per_slot = np.arange(ulysses_count) * per_device // group_width
    key_outgoing = key_state_rows.reshape(token_rows, KEY_VALUE_HEADS, HEAD_SIZE)[
        :, heads_per_slot
    ].reshape(token_rows, ulysses_count * HEAD_SIZE)
    value_outgoing = value_state_rows.reshape(token_rows, KEY_VALUE_HEADS, HEAD_SIZE)[
        :, heads_per_slot
    ].reshape(token_rows, ulysses_count * HEAD_SIZE)
    q_group, k_group, v_group = (
        lax.all_to_all(queries, "uly", split_axis=1, concat_axis=0, tiled=True),
        lax.all_to_all(key_outgoing, "uly", split_axis=1, concat_axis=0, tiled=True),
        lax.all_to_all(value_outgoing, "uly", split_axis=1, concat_axis=0, tiled=True),
    )
    seg_rows = q_group.shape[0]
    block_count = seg_rows // BLOCK_TOKENS
    reach = block_count // 2
    q_tiles = q_group.reshape(block_count, BLOCK_TOKENS, per_device, HEAD_SIZE)
    key_block_tiles = k_group.reshape(block_count, BLOCK_TOKENS, HEAD_SIZE)
    value_block_tiles = v_group.reshape(block_count, BLOCK_TOKENS, HEAD_SIZE)
    prior_k, prior_v = passed_along(
        (key_block_tiles[block_count - reach :], value_block_tiles[block_count - reach :]), "grp", 1
    )
    k_wide = jnp.concatenate([prior_k, key_block_tiles], axis=0)
    v_wide = jnp.concatenate([prior_v, value_block_tiles], axis=0)
    heads_here = lax.dynamic_slice_in_dim(ordering, uly_id * per_device, per_device)
    vert_list = jnp.take(vert_blocks, heads_here, axis=0)
    offset_list = jnp.take(slash_offsets, heads_here, axis=0)
    local_block = jnp.where(vert_list >= 0, vert_list % block_count, 0)
    owned = (vert_list >= 0) & (vert_list // block_count == group_id)
    pick_k = jnp.where(
        owned[:, :, None, None], key_block_tiles[local_block], jnp.zeros((), jnp.bfloat16)
    )
    pick_v = jnp.where(
        owned[:, :, None, None], value_block_tiles[local_block], jnp.zeros((), jnp.bfloat16)
    )
    summed_k, summed_v = (
        lax.psum(pick_k.astype(jnp.float32).astype(jnp.bfloat16), "grp").astype(jnp.float32),
        lax.psum(pick_v.astype(jnp.float32).astype(jnp.bfloat16), "grp").astype(jnp.float32),
    )
    vert_k = summed_k.astype(jnp.bfloat16)
    vert_v = summed_v.astype(jnp.bfloat16)
    query_blocks = group_id * block_count + jnp.arange(block_count, dtype=jnp.int32)
    score_scale = HEAD_SIZE ** (-0.5)
    causal = (jnp.arange(BLOCK_TOKENS)[:, None] >= jnp.arange(BLOCK_TOKENS)[None, :])[
        None, :, None, :
    ]
    diag_scores = (
        jnp.einsum("nqhd,nkd->nqhk", q_tiles, key_block_tiles, preferred_element_type=jnp.float32)
        * score_scale
    )
    diag_scores = jnp.where(causal, diag_scores, neg_large)
    best = jnp.max(diag_scores, axis=-1)
    diag_weights = jnp.where(causal, jnp.exp(diag_scores - best[..., None]), 0.0)
    total = jnp.sum(diag_weights, axis=-1)
    accum = jnp.einsum(
        "nqhk,nkd->nqhd",
        diag_weights.astype(jnp.bfloat16),
        value_block_tiles,
        preferred_element_type=jnp.float32,
    )
    running = (best, total, accum)

    def slash_slot(slot_index, running):
        offset_now = lax.dynamic_index_in_dim(offset_list, slot_index, axis=1, keepdims=False)
        starts = jnp.where(offset_now >= 1, reach - offset_now, 0)

        def near_slice(begin_at):
            return (
                lax.dynamic_slice_in_dim(k_wide, begin_at, block_count, 0),
                lax.dynamic_slice_in_dim(v_wide, begin_at, block_count, 0),
            )

        k_near, v_near = jax.vmap(near_slice)(starts)
        allowed = (offset_now[None, :] >= 1) & (query_blocks[:, None] - offset_now[None, :] >= 0)
        slot_scores = (
            jnp.einsum("nqhd,hnkd->nqhk", q_tiles, k_near, preferred_element_type=jnp.float32)
            * score_scale
        )

        def weigh_near(prob_low):
            return jnp.einsum(
                "nqhk,hnkd->nqhd", prob_low, v_near, preferred_element_type=jnp.float32
            )

        return add_slot(running, slot_scores, allowed[:, None, :, None], weigh_near)

    slash_turns = jnp.max(jnp.sum((offset_list >= 1).astype(jnp.int32), axis=1))
    running = lax.fori_loop(0, slash_turns, slash_slot, running)

    def vert_slot(slot_index, running):
        block_now = lax.dynamic_index_in_dim(vert_list, slot_index, axis=1, keepdims=False)
        k_far = lax.dynamic_index_in_dim(vert_k, slot_index, axis=1, keepdims=False)
        v_far = lax.dynamic_index_in_dim(vert_v, slot_index, axis=1, keepdims=False)
        hits = (offset_list[None, :, :] >= 1) & (
            query_blocks[:, None, None] - offset_list[None, :, :] == block_now[None, :, None]
        )
        allowed = (
            (block_now[None, :] >= 0)
            & (block_now[None, :] < query_blocks[:, None])
            & jnp.logical_not(jnp.any(hits, axis=2))
        )
        slot_scores = (
            jnp.einsum("nqhd,hkd->nqhk", q_tiles, k_far, preferred_element_type=jnp.float32)
            * score_scale
        )

        def weigh_far(prob_low):
            return jnp.einsum("nqhk,hkd->nqhd", prob_low, v_far, preferred_element_type=jnp.float32)

        return add_slot(running, slot_scores, allowed[:, None, :, None], weigh_far)

    vert_turns = jnp.max(jnp.sum((vert_list >= 0).astype(jnp.int32), axis=1))
    best, total, accum = lax.fori_loop(0, vert_turns, vert_slot, running)
    mixed = (
        (accum / total[..., None]).astype(jnp.bfloat16).reshape(seg_rows, per_device * HEAD_SIZE)
    )
    returned = lax.all_to_all(mixed, "uly", split_axis=0, concat_axis=1, tiled=True)
    return returned


MESH = pl.DeviceIdType.MESH
GATHERED_BYTES_MAX = 1 << 25
LOG2_E = 1.4426950408889634
EARLY = ("zyx", "zxy")
LATE = ("yzx", "xzy")


def orders_of(head):
    return LATE if head % 3 == 1 else EARLY


def place_in(order, sizes, where):
    place = where["core"]
    for axis in reversed(order):
        place = place * sizes[axis] + where[axis]
    return place


def sizes_of(group_count, uly_count):
    return {"x": group_count // 2, "core": 2, "y": 2, "z": uly_count // 2}


def whereabouts(group, member):
    return {"x": group // 2, "core": group % 2, "y": member % 2, "z": member // 2}


def place_table(group_count, uly_count):
    block = np.arange(group_count * uly_count)
    where = whereabouts(block // uly_count, block % uly_count)
    sizes = sizes_of(group_count, uly_count)
    rows = [place_in(order, sizes, where) for order in EARLY + LATE]
    return np.stack(rows).astype(np.int32)


def attend_all(orders, q_ref, k_buf, v_buf, place_ref, vert_ref, slash_ref, out_ref, head, here):
    per_group = q_ref.shape[1] // (HEAD_SIZE * KEY_VALUE_HEADS)
    slash_slots, vert_slots = slash_ref.shape[0], vert_ref.shape[0]
    rate = HEAD_SIZE ** (-0.5) * LOG2_E
    causal = lax.broadcasted_iota(
        jnp.int32, (BLOCK_TOKENS, BLOCK_TOKENS), 0
    ) >= lax.broadcasted_iota(jnp.int32, (BLOCK_TOKENS, BLOCK_TOKENS), 1)
    k_row, v_row = ((EARLY + LATE).index(order) for order in orders)

    def slots_of(q_head):
        blocks, allowed = [here], [None]
        offsets = [slash_ref[slot, q_head] for slot in range(slash_slots)]
        for offset in offsets:
            ok = (offset >= 1) & (here - offset >= 0)
            blocks.append(jnp.where(ok, here - offset, here))
            allowed.append(ok)
        for slot in range(vert_slots):
            block = vert_ref[slot, q_head]
            ok = (block >= 0) & (block < here)
            for offset in offsets:
                ok = ok & jnp.logical_not((offset >= 1) & (here - offset == block))
            blocks.append(jnp.where(ok, block, here))
            allowed.append(ok)
        return blocks, allowed

    @pl.loop(0, per_group // GANG)
    def _(turn):
        chosen_slots, columns, scores = [], [], []
        for n in range(GANG):
            q_head = head * per_group + GANG * turn + n
            columns.append(pl.ds(pl.multiple_of(q_head * HEAD_SIZE, HEAD_SIZE), HEAD_SIZE))
            chosen_slots.append(slots_of(q_head))
        for n in range(GANG):
            blocks, _ = chosen_slots[n]
            keys = jnp.concatenate([k_buf[place_ref[k_row, block]] for block in blocks], axis=0)
            scores.append(
                lax.dot_general(
                    q_ref[:, columns[n]],
                    keys,
                    (((1,), (1,)), ((), ())),
                    preferred_element_type=jnp.float32,
                )
            )
        probs, totals = [], []
        for n in range(GANG):
            _, allowed = chosen_slots[n]
            pieces = []
            for slot, ok in enumerate(allowed):
                piece = scores[n][:, slot * BLOCK_TOKENS : (slot + 1) * BLOCK_TOKENS]
                if ok is None:
                    pieces.append(jnp.where(causal, piece, neg_large))
                else:
                    pieces.append(piece + jnp.where(ok, 0.0, neg_large).astype(jnp.float32))
            best = functools.reduce(jnp.maximum, pieces)
            best = jnp.max(best, axis=1, keepdims=True)
            weights = [jnp.exp2((piece - best) * rate) for piece in pieces]
            total = functools.reduce(jnp.add, weights)
            totals.append(jnp.sum(total, axis=1, keepdims=True))
            probs.append(
                jnp.concatenate([weight.astype(jnp.bfloat16) for weight in weights], axis=1)
            )
        for n in range(GANG):
            blocks, _ = chosen_slots[n]
            values = jnp.concatenate([v_buf[place_ref[v_row, block]] for block in blocks], axis=0)
            mixed = jnp.dot(probs[n], values, preferred_element_type=jnp.float32)
            out_ref[:, columns[n]] = (mixed / totals[n]).astype(out_ref.dtype)


GANG = 4
AHEAD = 2


def resident_kernel(
    group_count,
    uly_count,
    place_ref,
    vert_ref,
    slash_ref,
    q_ref,
    k_ref,
    v_ref,
    out_ref,
    own_sem,
    send_sem,
    recv_sem,
    *held,
):
    sizes = sizes_of(group_count, uly_count)
    group, member = lax.axis_index("grp"), lax.axis_index("uly")
    me = whereabouts(group, member)
    here = group * uly_count + member
    heads = KEY_VALUE_HEADS

    def device_at(where):
        return (where["x"] * 2 + where["core"], where["z"] * 2 + where["y"])

    peers, first, used = {}, {}, 0
    for axis in ("x", "y", "z", "core"):
        count = sizes[axis]
        peers[axis] = [
            device_at({**me, axis: lax.rem(me[axis] + d, count)}) for d in range(1, count)
        ]
        first[axis] = used
        used += count - 1

    barrier = pltpu.get_barrier_semaphore()
    everyone = [peer for group_peers in peers.values() for peer in group_peers]
    for peer in everyone:
        pl.semaphore_signal(barrier, inc=1, device_id=peer, device_id_type=MESH)
    pl.semaphore_wait(barrier, len(everyone))

    all_copies = []

    def sent(source, target, item, axis):
        copies = []
        for n, peer in enumerate(peers[axis]):
            copy = pltpu.make_async_remote_copy(
                src_ref=source,
                dst_ref=target,
                send_sem=send_sem.at[item, first[axis] + n],
                recv_sem=recv_sem.at[item, first[axis] + n],
                device_id=peer,
                device_id_type=MESH,
            )
            copy.start()
            copies.append(copy)
        all_copies.extend(copies)
        return copies

    flights, own = {}, {}

    def begin(head):
        for kind, source in enumerate((k_ref, v_ref)):
            item, order = 2 * head + kind, orders_of(head)[kind]
            slot = held[item].at[place_in(order, sizes, me)]
            columns = source.at[:, pl.ds(head * HEAD_SIZE, HEAD_SIZE)]
            flights[item] = sent(columns, slot, item, order[0])
            own[item] = pltpu.make_async_copy(columns, slot, own_sem.at[item])
            own[item].start()

    for head in range(min(AHEAD, heads)):
        begin(head)

    def forward(head, stage):
        for kind in range(2):
            item, order = 2 * head + kind, orders_of(head)[kind]
            if stage == 1:
                own[item].wait()
            for copy in flights[item]:
                copy.wait_recv()
            if stage <= 3:
                route = [*order, "core"]
                start = {**me, **{axis: 0 for axis in route[:stage]}}
                count = 1
                for axis in route[:stage]:
                    count *= sizes[axis]
                slab = held[item].at[pl.ds(place_in(order, sizes, start), count)]
                flights[item] = sent(slab, slab, item, route[stage])

    for step in range(heads + 3):
        if step + AHEAD < heads:
            begin(step + AHEAD)
        if step < heads:
            forward(step, 1)
        if 0 <= step - 1 < heads:
            forward(step - 1, 2)
        if 0 <= step - 3 < heads:
            head = step - 3
            forward(head, 4)
            attend_all(
                orders_of(head),
                q_ref,
                held[2 * head],
                held[2 * head + 1],
                place_ref,
                vert_ref,
                slash_ref,
                out_ref,
                head,
                here,
            )
        if 0 <= step - 2 < heads:
            forward(step - 2, 3)
    for copy in all_copies:
        copy.wait_send()


def resident_shards(queries, key_state_rows, value_state_rows, vert_blocks, slash_offsets):
    group_count, uly_count = lax.axis_size("grp"), lax.axis_size("uly")
    sizes = sizes_of(group_count, uly_count)
    copies = sum(count - 1 for count in sizes.values())
    items = 2 * KEY_VALUE_HEADS
    blocks = group_count * uly_count
    vmem = pl.BlockSpec(memory_space=pltpu.VMEM)
    smem = pl.BlockSpec(memory_space=pltpu.SMEM)
    return pl.pallas_call(
        functools.partial(resident_kernel, group_count, uly_count),
        out_shape=jax.ShapeDtypeStruct(queries.shape, queries.dtype),
        in_specs=[smem, smem, smem, vmem, vmem, vmem],
        out_specs=vmem,
        scratch_shapes=[
            pltpu.SemaphoreType.DMA((items,)),
            pltpu.SemaphoreType.DMA((items, copies)),
            pltpu.SemaphoreType.DMA((items, copies)),
        ]
        + [pltpu.VMEM((blocks, BLOCK_TOKENS, HEAD_SIZE), key_state_rows.dtype)] * items,
        compiler_params=pltpu.CompilerParams(collective_id=0, has_side_effects=True),
        name="gather_and_attend",
    )(
        jnp.asarray(place_table(group_count, uly_count)),
        vert_blocks.T,
        slash_offsets.T,
        queries,
        key_state_rows,
        value_state_rows,
    )


def chosen(queries, key_state_rows, *rest):
    devices = lax.axis_size("grp") * lax.axis_size("uly")
    gathered_bytes = 2 * devices * key_state_rows.size * key_state_rows.dtype.itemsize
    fits = gathered_bytes <= GATHERED_BYTES_MAX and queries.shape[0] == BLOCK_TOKENS
    plan = resident_shards if fits else shards
    return plan(queries, key_state_rows, *rest)


def solution(mesh):
    return jax.shard_map(
        chosen,
        mesh=mesh,
        in_specs=(
            P(("grp", "uly"), None),
            P(("grp", "uly"), None),
            P(("grp", "uly"), None),
            P(),
            P(),
        ),
        out_specs=P(("grp", "uly"), None),
        check_vma=False,
    )
```

```python
import functools

import jax
import jax.numpy as jnp
import numpy as np
from jax import lax
from jax.experimental import pallas as pl
from jax.experimental.pallas import tpu as pltpu
from jax.sharding import PartitionSpec as P

QUERY_HEADS = 64
KEY_VALUE_HEADS = 8
HEAD_SIZE = 128
BLOCK_TOKENS = 128


neg_large = -1e30


def passed_along(value, axis, steps):
    count = lax.axis_size(axis)
    initial, last = (max(0, -steps), min(count, count - steps))
    return lax.ppermute(value, axis, [(source, source + steps) for source in range(initial, last)])


def add_slot(running, slot_scores, allowed, weigh):
    best, total, accum = running
    slot_scores = jnp.where(allowed, slot_scores, neg_large)
    new_best = jnp.maximum(best, jnp.max(slot_scores, axis=-1))
    factor = jnp.exp(best - new_best)
    weights = jnp.where(allowed, jnp.exp(slot_scores - new_best[..., None]), 0.0)
    total = total * factor + jnp.sum(weights, axis=-1)
    accum = accum * factor[..., None] + weigh(weights.astype(jnp.bfloat16))
    return (new_best, total, accum)


def shards(queries, key_state_rows, value_state_rows, vert_blocks, slash_offsets):
    ulysses_count = lax.axis_size("uly")
    group_id = lax.axis_index("grp")
    uly_id = lax.axis_index("uly")
    per_device = QUERY_HEADS // ulysses_count
    group_width = QUERY_HEADS // KEY_VALUE_HEADS
    token_rows = queries.shape[0]
    ordering = jnp.arange(QUERY_HEADS, dtype=jnp.int32)
    heads_per_slot = np.arange(ulysses_count) * per_device // group_width
    key_outgoing = key_state_rows.reshape(token_rows, KEY_VALUE_HEADS, HEAD_SIZE)[
        :, heads_per_slot
    ].reshape(token_rows, ulysses_count * HEAD_SIZE)
    value_outgoing = value_state_rows.reshape(token_rows, KEY_VALUE_HEADS, HEAD_SIZE)[
        :, heads_per_slot
    ].reshape(token_rows, ulysses_count * HEAD_SIZE)
    q_group, k_group, v_group = (
        lax.all_to_all(queries, "uly", split_axis=1, concat_axis=0, tiled=True),
        lax.all_to_all(key_outgoing, "uly", split_axis=1, concat_axis=0, tiled=True),
        lax.all_to_all(value_outgoing, "uly", split_axis=1, concat_axis=0, tiled=True),
    )
    seg_rows = q_group.shape[0]
    block_count = seg_rows // BLOCK_TOKENS
    reach = block_count // 2
    q_tiles = q_group.reshape(block_count, BLOCK_TOKENS, per_device, HEAD_SIZE)
    key_block_tiles = k_group.reshape(block_count, BLOCK_TOKENS, HEAD_SIZE)
    value_block_tiles = v_group.reshape(block_count, BLOCK_TOKENS, HEAD_SIZE)
    prior_k, prior_v = passed_along(
        (key_block_tiles[block_count - reach :], value_block_tiles[block_count - reach :]), "grp", 1
    )
    k_wide = jnp.concatenate([prior_k, key_block_tiles], axis=0)
    v_wide = jnp.concatenate([prior_v, value_block_tiles], axis=0)
    heads_here = lax.dynamic_slice_in_dim(ordering, uly_id * per_device, per_device)
    vert_list = jnp.take(vert_blocks, heads_here, axis=0)
    offset_list = jnp.take(slash_offsets, heads_here, axis=0)
    local_block = jnp.where(vert_list >= 0, vert_list % block_count, 0)
    owned = (vert_list >= 0) & (vert_list // block_count == group_id)
    pick_k = jnp.where(
        owned[:, :, None, None], key_block_tiles[local_block], jnp.zeros((), jnp.bfloat16)
    )
    pick_v = jnp.where(
        owned[:, :, None, None], value_block_tiles[local_block], jnp.zeros((), jnp.bfloat16)
    )
    summed_k, summed_v = (
        lax.psum(pick_k.astype(jnp.float32).astype(jnp.bfloat16), "grp").astype(jnp.float32),
        lax.psum(pick_v.astype(jnp.float32).astype(jnp.bfloat16), "grp").astype(jnp.float32),
    )
    vert_k = summed_k.astype(jnp.bfloat16)
    vert_v = summed_v.astype(jnp.bfloat16)
    query_blocks = group_id * block_count + jnp.arange(block_count, dtype=jnp.int32)
    score_scale = HEAD_SIZE ** (-0.5)
    causal = (jnp.arange(BLOCK_TOKENS)[:, None] >= jnp.arange(BLOCK_TOKENS)[None, :])[
        None, :, None, :
    ]
    diag_scores = (
        jnp.einsum("nqhd,nkd->nqhk", q_tiles, key_block_tiles, preferred_element_type=jnp.float32)
        * score_scale
    )
    diag_scores = jnp.where(causal, diag_scores, neg_large)
    best = jnp.max(diag_scores, axis=-1)
    diag_weights = jnp.where(causal, jnp.exp(diag_scores - best[..., None]), 0.0)
    total = jnp.sum(diag_weights, axis=-1)
    accum = jnp.einsum(
        "nqhk,nkd->nqhd",
        diag_weights.astype(jnp.bfloat16),
        value_block_tiles,
        preferred_element_type=jnp.float32,
    )
    running = (best, total, accum)

    def slash_slot(slot_index, running):
        offset_now = lax.dynamic_index_in_dim(offset_list, slot_index, axis=1, keepdims=False)
        starts = jnp.where(offset_now >= 1, reach - offset_now, 0)

        def near_slice(begin_at):
            return (
                lax.dynamic_slice_in_dim(k_wide, begin_at, block_count, 0),
                lax.dynamic_slice_in_dim(v_wide, begin_at, block_count, 0),
            )

        k_near, v_near = jax.vmap(near_slice)(starts)
        allowed = (offset_now[None, :] >= 1) & (query_blocks[:, None] - offset_now[None, :] >= 0)
        slot_scores = (
            jnp.einsum("nqhd,hnkd->nqhk", q_tiles, k_near, preferred_element_type=jnp.float32)
            * score_scale
        )

        def weigh_near(prob_low):
            return jnp.einsum(
                "nqhk,hnkd->nqhd", prob_low, v_near, preferred_element_type=jnp.float32
            )

        return add_slot(running, slot_scores, allowed[:, None, :, None], weigh_near)

    slash_turns = jnp.max(jnp.sum((offset_list >= 1).astype(jnp.int32), axis=1))
    running = lax.fori_loop(0, slash_turns, slash_slot, running)

    def vert_slot(slot_index, running):
        block_now = lax.dynamic_index_in_dim(vert_list, slot_index, axis=1, keepdims=False)
        k_far = lax.dynamic_index_in_dim(vert_k, slot_index, axis=1, keepdims=False)
        v_far = lax.dynamic_index_in_dim(vert_v, slot_index, axis=1, keepdims=False)
        hits = (offset_list[None, :, :] >= 1) & (
            query_blocks[:, None, None] - offset_list[None, :, :] == block_now[None, :, None]
        )
        allowed = (
            (block_now[None, :] >= 0)
            & (block_now[None, :] < query_blocks[:, None])
            & jnp.logical_not(jnp.any(hits, axis=2))
        )
        slot_scores = (
            jnp.einsum("nqhd,hkd->nqhk", q_tiles, k_far, preferred_element_type=jnp.float32)
            * score_scale
        )

        def weigh_far(prob_low):
            return jnp.einsum("nqhk,hkd->nqhd", prob_low, v_far, preferred_element_type=jnp.float32)

        return add_slot(running, slot_scores, allowed[:, None, :, None], weigh_far)

    vert_turns = jnp.max(jnp.sum((vert_list >= 0).astype(jnp.int32), axis=1))
    best, total, accum = lax.fori_loop(0, vert_turns, vert_slot, running)
    mixed = (
        (accum / total[..., None]).astype(jnp.bfloat16).reshape(seg_rows, per_device * HEAD_SIZE)
    )
    returned = lax.all_to_all(mixed, "uly", split_axis=0, concat_axis=1, tiled=True)
    return returned


MESH = pl.DeviceIdType.MESH
GATHERED_BYTES_MAX = 1 << 25
LOG2_E = 1.4426950408889634
EARLY = ("zyx", "zxy")
LATE = ("yzx", "xzy")


def orders_of(head):
    return LATE if head % 3 == 1 else EARLY


def place_in(order, sizes, where):
    place = where["core"]
    for axis in reversed(order):
        place = place * sizes[axis] + where[axis]
    return place


def sizes_of(group_count, uly_count):
    return {"x": group_count // 2, "core": 2, "y": 2, "z": uly_count // 2}


def whereabouts(group, member):
    return {"x": group // 2, "core": group % 2, "y": member % 2, "z": member // 2}


def place_table(group_count, uly_count):
    block = np.arange(group_count * uly_count)
    where = whereabouts(block // uly_count, block % uly_count)
    sizes = sizes_of(group_count, uly_count)
    rows = [place_in(order, sizes, where) for order in EARLY + LATE]
    return np.stack(rows).astype(np.int32)


def attend_all(orders, q_ref, k_buf, v_buf, place_ref, vert_ref, slash_ref, out_ref, head, here):
    per_group = q_ref.shape[1] // (HEAD_SIZE * KEY_VALUE_HEADS)
    slash_slots, vert_slots = slash_ref.shape[0], vert_ref.shape[0]
    rate = HEAD_SIZE ** (-0.5) * LOG2_E
    causal = lax.broadcasted_iota(
        jnp.int32, (BLOCK_TOKENS, BLOCK_TOKENS), 0
    ) >= lax.broadcasted_iota(jnp.int32, (BLOCK_TOKENS, BLOCK_TOKENS), 1)
    k_row, v_row = ((EARLY + LATE).index(order) for order in orders)

    def slots_of(q_head):
        blocks, allowed = [here], [None]
        offsets = [slash_ref[slot, q_head] for slot in range(slash_slots)]
        for offset in offsets:
            ok = (offset >= 1) & (here - offset >= 0)
            blocks.append(jnp.where(ok, here - offset, here))
            allowed.append(ok)
        for slot in range(vert_slots):
            block = vert_ref[slot, q_head]
            ok = (block >= 0) & (block < here)
            for offset in offsets:
                ok = ok & jnp.logical_not((offset >= 1) & (here - offset == block))
            blocks.append(jnp.where(ok, block, here))
            allowed.append(ok)
        return blocks, allowed

    @pl.loop(0, per_group // GANG)
    def _(turn):
        chosen_slots, columns, scores = [], [], []
        for n in range(GANG):
            q_head = head * per_group + GANG * turn + n
            columns.append(pl.ds(pl.multiple_of(q_head * HEAD_SIZE, HEAD_SIZE), HEAD_SIZE))
            chosen_slots.append(slots_of(q_head))
        for n in range(GANG):
            blocks, _ = chosen_slots[n]
            keys = jnp.concatenate([k_buf[place_ref[k_row, block]] for block in blocks], axis=0)
            scores.append(
                lax.dot_general(
                    q_ref[:, columns[n]],
                    keys,
                    (((1,), (1,)), ((), ())),
                    preferred_element_type=jnp.float32,
                )
            )
        probs, totals = [], []
        for n in range(GANG):
            _, allowed = chosen_slots[n]
            pieces = []
            for slot, ok in enumerate(allowed):
                piece = scores[n][:, slot * BLOCK_TOKENS : (slot + 1) * BLOCK_TOKENS]
                if ok is None:
                    pieces.append(jnp.where(causal, piece, neg_large))
                else:
                    pieces.append(piece + jnp.where(ok, 0.0, neg_large).astype(jnp.float32))
            best = functools.reduce(jnp.maximum, pieces)
            best = jnp.max(best, axis=1, keepdims=True)
            weights = [jnp.exp2((piece - best) * rate) for piece in pieces]
            total = functools.reduce(jnp.add, weights)
            totals.append(jnp.sum(total, axis=1, keepdims=True))
            probs.append(
                jnp.concatenate([weight.astype(jnp.bfloat16) for weight in weights], axis=1)
            )
        for n in range(GANG):
            blocks, _ = chosen_slots[n]
            values = jnp.concatenate([v_buf[place_ref[v_row, block]] for block in blocks], axis=0)
            mixed = jnp.dot(probs[n], values, preferred_element_type=jnp.float32)
            out_ref[:, columns[n]] = (mixed / totals[n]).astype(out_ref.dtype)


GANG = 4
AHEAD = 1


def resident_kernel(
    group_count,
    uly_count,
    place_ref,
    vert_ref,
    slash_ref,
    q_hbm,
    k_ref,
    v_ref,
    out_hbm,
    q_ref,
    out_ref,
    q_sem,
    out_sem,
    own_sem,
    send_sem,
    recv_sem,
    *held,
):
    sizes = sizes_of(group_count, uly_count)
    group, member = lax.axis_index("grp"), lax.axis_index("uly")
    me = whereabouts(group, member)
    here = group * uly_count + member
    heads = KEY_VALUE_HEADS
    per_head = q_hbm.shape[1] // heads
    q_copy = pltpu.make_async_copy(q_hbm, q_ref, q_sem)
    q_copy.start()
    out_copies = []

    def device_at(where):
        return (where["x"] * 2 + where["core"], where["z"] * 2 + where["y"])

    peers, first, used = {}, {}, 0
    for axis in ("x", "y", "z", "core"):
        count = sizes[axis]
        peers[axis] = [
            device_at({**me, axis: lax.rem(me[axis] + d, count)}) for d in range(1, count)
        ]
        first[axis] = used
        used += count - 1

    barrier = pltpu.get_barrier_semaphore()
    everyone = [peer for group_peers in peers.values() for peer in group_peers]
    for peer in everyone:
        pl.semaphore_signal(barrier, inc=1, device_id=peer, device_id_type=MESH)
    pl.semaphore_wait(barrier, len(everyone))

    all_copies = []

    def sent(source, target, item, axis):
        copies = []
        for n, peer in enumerate(peers[axis]):
            copy = pltpu.make_async_remote_copy(
                src_ref=source,
                dst_ref=target,
                send_sem=send_sem.at[item, first[axis] + n],
                recv_sem=recv_sem.at[item, first[axis] + n],
                device_id=peer,
                device_id_type=MESH,
            )
            copy.start()
            copies.append(copy)
        all_copies.extend(copies)
        return copies

    flights, own = {}, {}

    def begin(head):
        for kind, source in enumerate((k_ref, v_ref)):
            item, order = 2 * head + kind, orders_of(head)[kind]
            slot = held[item].at[place_in(order, sizes, me)]
            columns = source.at[:, pl.ds(head * HEAD_SIZE, HEAD_SIZE)]
            flights[item] = sent(columns, slot, item, order[0])
            own[item] = pltpu.make_async_copy(columns, slot, own_sem.at[item])
            own[item].start()

    def forward(head, stage):
        for kind in range(2):
            item, order = 2 * head + kind, orders_of(head)[kind]
            if stage == 1:
                own[item].wait()
            for copy in flights[item]:
                copy.wait_recv()
            if stage <= 3:
                route = [*order, "core"]
                start = {**me, **{axis: 0 for axis in route[:stage]}}
                count = 1
                for axis in route[:stage]:
                    count *= sizes[axis]
                slab = held[item].at[pl.ds(place_in(order, sizes, start), count)]
                flights[item] = sent(slab, slab, item, route[stage])

    def along_z(head):
        if orders_of(head) == LATE:
            forward(head, 1)
        else:
            begin(head)

    for head in range(heads):
        if orders_of(head) == LATE:
            begin(head)
    for head in range(min(AHEAD, heads)):
        along_z(head)
    for step in range(heads + 3):
        if step + AHEAD < heads:
            along_z(step + AHEAD)
        if step < heads and orders_of(step) == EARLY:
            forward(step, 1)
        if 0 <= step - 1 < heads:
            forward(step - 1, 2)
        if 0 <= step - 3 < heads:
            head = step - 3
            forward(head, 4)
            if head == 0:
                q_copy.wait()
            attend_all(
                orders_of(head),
                q_ref,
                held[2 * head],
                held[2 * head + 1],
                place_ref,
                vert_ref,
                slash_ref,
                out_ref,
                head,
                here,
            )
            columns = pl.ds(head * per_head, per_head)
            out_copies.append(
                pltpu.make_async_copy(
                    out_ref.at[:, columns], out_hbm.at[:, columns], out_sem.at[head]
                )
            )
            out_copies[-1].start()
        if 0 <= step - 2 < heads:
            forward(step - 2, 3)
    for copy in all_copies:
        copy.wait_send()
    for copy in out_copies:
        copy.wait()


def resident_shards(queries, key_state_rows, value_state_rows, vert_blocks, slash_offsets):
    group_count, uly_count = lax.axis_size("grp"), lax.axis_size("uly")
    sizes = sizes_of(group_count, uly_count)
    copies = sum(count - 1 for count in sizes.values())
    items = 2 * KEY_VALUE_HEADS
    blocks = group_count * uly_count
    vmem = pl.BlockSpec(memory_space=pltpu.VMEM)
    smem = pl.BlockSpec(memory_space=pltpu.SMEM)
    hbm = pl.BlockSpec(memory_space=pl.ANY)
    return pl.pallas_call(
        functools.partial(resident_kernel, group_count, uly_count),
        out_shape=jax.ShapeDtypeStruct(queries.shape, queries.dtype),
        in_specs=[smem, smem, smem, hbm, vmem, vmem],
        out_specs=hbm,
        scratch_shapes=[
            pltpu.VMEM(queries.shape, queries.dtype),
            pltpu.VMEM(queries.shape, queries.dtype),
            pltpu.SemaphoreType.DMA,
            pltpu.SemaphoreType.DMA((KEY_VALUE_HEADS,)),
            pltpu.SemaphoreType.DMA((items,)),
            pltpu.SemaphoreType.DMA((items, copies)),
            pltpu.SemaphoreType.DMA((items, copies)),
        ]
        + [pltpu.VMEM((blocks, BLOCK_TOKENS, HEAD_SIZE), key_state_rows.dtype)] * items,
        compiler_params=pltpu.CompilerParams(collective_id=0, has_side_effects=True),
        name="gather_and_attend",
    )(
        jnp.asarray(place_table(group_count, uly_count)),
        vert_blocks.T,
        slash_offsets.T,
        queries,
        key_state_rows,
        value_state_rows,
    )


def chosen(queries, key_state_rows, *rest):
    devices = lax.axis_size("grp") * lax.axis_size("uly")
    gathered_bytes = 2 * devices * key_state_rows.size * key_state_rows.dtype.itemsize
    fits = gathered_bytes <= GATHERED_BYTES_MAX and queries.shape[0] == BLOCK_TOKENS
    plan = resident_shards if fits else shards
    return plan(queries, key_state_rows, *rest)


def solution(mesh):
    return jax.shard_map(
        chosen,
        mesh=mesh,
        in_specs=(
            P(("grp", "uly"), None),
            P(("grp", "uly"), None),
            P(("grp", "uly"), None),
            P(),
            P(),
        ),
        out_specs=P(("grp", "uly"), None),
        check_vma=False,
    )
```
